256 devices in a mesh: frame: 8 (over x, core), cell: 32 (over z, y).
Axes of the slice: x: 4, y: 4, z: 8, core: 2. Of those that a mesh axis runs over, the one named last changes fastest.
Arguments:
- a_blocks: bfloat16 [4096, 64, 384], P(('frame', 'cell')), may hold values from -0.3125 to 0.3125
- a_cols: int32 [4096, 6], P(('frame', 'cell')), may hold values from 0 to 4095, as said below
- p_blocks: bfloat16 [4096, 64, 128], P(('frame', 'cell')), may hold values from -2 to 2
- p_cells: int32 [4096, 2], P(('frame', 'cell')), may hold values from 0 to 31, all different within a row; in each aligned block of 16 rows (0 to 15, 16 to 31, ...) at most 2 rows name the same one
Outputs:
- coarse_blocks: bfloat16 [512, 3, 3, 64, 2048], P(('frame', 'cell'))
The draws below stay inside these ranges and needn't reach their ends.
Inputs may be any that keep to these rules, and one draw needn't show every extreme that they name: a_cols[g, 0] = g. Every other stored block names a fine row of the same cell group, in the same or an adjacent frame range, whose local row differs from g's by at most 8; at most one of them lies in the previous and at most one in the next frame range. `p_cells`: the cells named in one row differ. Among the rows of one device, no cell is named more than 2 times, a bound that some block reaches.
All inputs are finite; a program needn't handle non-finite values.
Results may differ from the reference program's by a relative error of at most 0.0049.
Values may be sent and summed in bfloat16 or wider, within the bound.
No kernel may reach another device: no remote copies, remote signals or barrier semaphores. Data moves between devices by JAX's collectives and lax.ppermute only.
A program may use at most 192 MiB of HBM per device.

```python
import math
import jax
import jax.numpy as jnp
import numpy as np
from jax import lax

BS = 64
NNZ_A = 6
NNZ_P = 2
AGG = 8
ROWS_DEV = 16
NCR_DEV = 2
CAP = 2
NF = 4096
N_FRAME = 8
N_CELL = 32


def draw_a_cols(key, part):
    total = ROWS_DEV * N_FRAME * N_CELL
    rows = jnp.arange(total, dtype=jnp.int32)
    local = rows % ROWS_DEV
    frame = rows // (ROWS_DEV * N_CELL)
    offsets = jax.random.randint(key, (total, NNZ_A), -AGG, AGG + 1).astype(jnp.int32)
    target = jnp.clip(local[:, None] + offsets, 0, ROWS_DEV - 1)
    slots = jnp.arange(NNZ_A, dtype=jnp.int32)
    step = jnp.where(slots == NNZ_A - 2, -1, jnp.where(slots == NNZ_A - 1, 1, 0)).astype(jnp.int32)
    moved = frame[:, None] + step[None, :]
    inside = (moved >= 0) & (moved < N_FRAME)
    step = jnp.where(inside, step[None, :], 0)
    base = rows - local
    cols = base[:, None] + step * (ROWS_DEV * N_CELL) + target
    cols = jnp.where(slots[None, :] == 0, rows[:, None], cols)
    return cols.astype(jnp.int32)


def block_scale(key, shape, pieces, smallest, high):
    factor_of = 1.0
    for dim, parts in pieces:
        steps = jax.random.uniform(jax.random.fold_in(jax.random.fold_in(key, 6), dim), (parts,), jnp.float32, smallest / len(pieces), high / len(pieces))
        factor_of = factor_of * jnp.repeat(jnp.exp(steps), shape[dim] // parts).reshape((-1,) + (1,) * (len(shape) - 1 - dim))
    return factor_of


def shared_out(rng, own, number, rows, count, top, limit, slope):
    order = jax.random.permutation(rng, count)
    packed, common = portions_of(count, rows * top, limit, slope, True), portions_of(count, rows * top, limit, slope, False)
    places = jnp.arange(count)

    def named(sizes, offset_by):
        used = int((sizes > 0).sum())
        fixed = max(1, used // 4)
        shifted = fixed + (places - fixed + offset_by * (used - fixed)) % max(1, count - fixed)
        return jnp.zeros((count,), jnp.int32).at[order[jnp.where(places < fixed, places, shifted)]].set(jnp.asarray(sizes, jnp.int32))

    sizes = jnp.where(number % 4 == 0, named(packed, number // 4), named(common, number - number // 4 - 1))
    mixed = jax.random.permutation(jax.random.fold_in(own, 3), count)
    donor, sink = mixed[0:count // 2 * 2:2], mixed[1:count // 2 * 2:2]
    slack = jnp.minimum(sizes[donor] - 1, limit - sizes[sink]) // 2
    slack = jnp.where((donor == order[0]) | (sink == order[0]) | (sizes[sink] == 0), 0, jnp.maximum(slack, 0))
    shifted = jax.random.randint(jax.random.fold_in(own, 4), (count // 2,), 0, 1 << 20) % (slack + 1)
    sizes = sizes.at[donor].add(-shifted).at[sink].add(shifted)
    members = jnp.searchsorted(jnp.cumsum(sizes), jnp.arange(rows * top), side="right").astype(jnp.int32)
    listing = members.reshape(top, rows).T
    listing = listing[jax.random.permutation(jax.random.fold_in(own, 1), rows)]
    offset_by = jax.random.randint(jax.random.fold_in(own, 2), (rows, 1), 0, top)
    return jnp.take_along_axis(listing, (jnp.arange(top)[None, :] + offset_by) % top, axis=1)


def portions_of(number_of, total, limit, slope, full):
    portions = [(1 << 20) // math.isqrt(rank ** slope) + 1 for rank in range(1, number_of + 1)]
    largest = limit if full else min(limit, max(-(-total // number_of), total * portions[0] // sum(portions)))
    least = 1 if total - largest >= number_of - 1 else 0
    given, surplus = [largest] + [least] * (number_of - 1), total - largest - least * (number_of - 1)
    while surplus > 0:
        candidates = [i for i in range(1, number_of) if given[i] < largest] or [i for i in range(1, number_of) if given[i] < limit]
        whole, left = sum([portions[i] for i in candidates]), surplus
        for i in candidates:
            more = min(limit - given[i], max(1, left * portions[i] // whole), surplus)
            given[i] = given[i] + more
            surplus = surplus - more
    return np.array(given)


def centred(stream_key, extent, width, reach, split=(), held_as=jnp.bfloat16):
    array = width * jax.random.normal(stream_key, extent, jnp.float32)
    if split:
        array = array * block_scale(stream_key, extent, split, -0.22, 0.18)
    return jnp.clip(array, -reach, reach).astype(held_as)


def setup_inputs(seed: int = 0) -> dict:
    arg_keys = jax.random.split(jax.random.key(seed), 5)
    a_blocks = centred(arg_keys[0], (NF, BS, NNZ_A * BS), (NNZ_A * BS) ** -0.5, 0.3125, ((0, 256),))
    a_cols = draw_a_cols(jax.random.fold_in(arg_keys[4], 71), 0)
    p_blocks = centred(arg_keys[2], (NF, BS, NNZ_P * BS), 0.35, 2.0, ((0, 256),))
    p_cells_keys = jax.random.split(jax.random.fold_in(arg_keys[3], 1), NF // ROWS_DEV)
    p_cells_turns = jax.random.permutation(jax.random.fold_in(arg_keys[3], 3), NF // ROWS_DEV)
    p_cells = jax.vmap(lambda own, number: shared_out(jax.random.fold_in(arg_keys[3], 2), own, number, ROWS_DEV, N_CELL, NNZ_P, CAP, 2))(p_cells_keys, p_cells_turns).reshape((NF, NNZ_P))
    return {"a_blocks": a_blocks, "a_cols": a_cols, "p_blocks": p_blocks, "p_cells": p_cells}


def reference(a_blocks, a_cols, p_blocks, p_cells):
    total = a_blocks.shape[0]
    a_four = a_blocks.reshape(total, BS, NNZ_A, BS)
    p_four = p_blocks.reshape(total, BS, NNZ_P, BS)
    per_frame = ROWS_DEV * N_CELL
    window = 9 * N_CELL
    coarse_rows = NCR_DEV * N_FRAME * N_CELL
    local_rows = jnp.arange(ROWS_DEV, dtype=jnp.int32)
    local_agg = local_rows // AGG

    def one_shard(carry, device):
        start = (device * ROWS_DEV).astype(jnp.int32)
        a_here = lax.dynamic_slice_in_dim(a_four, start, ROWS_DEV, 0)
        cols = lax.dynamic_slice_in_dim(a_cols, start, ROWS_DEV, 0)
        p_here = lax.dynamic_slice_in_dim(p_four, start, ROWS_DEV, 0)
        dest = lax.dynamic_slice_in_dim(p_cells, start, ROWS_DEV, 0)
        p_far = p_four[cols]
        cell_far = p_cells[cols]
        products = jnp.einsum('iakb,ikbpc->ikpac', a_here.astype(jnp.float32), p_far.astype(jnp.float32))
        products = lax.optimization_barrier(products.astype(jnp.bfloat16))
        terms = jnp.einsum('ibpa,ikqbc->ipkqac', p_here.astype(jnp.float32), products.astype(jnp.float32))
        frame = device // N_CELL
        offset_u = cols // per_frame - frame + 1
        offset_v = (cols % ROWS_DEV) // AGG - local_agg[:, None] + 1
        code = ((offset_u * 3 + offset_v)[:, :, None]) * N_CELL + cell_far
        owner = frame * N_CELL + dest
        target = (owner[:, :, None, None] * NCR_DEV + local_agg[:, None, None, None]) * window + code[:, None, :, :]
        carry = carry.at[target.reshape(-1)].add(terms.reshape(-1, BS, BS))
        return carry, None

    start_sum = jnp.zeros((coarse_rows * window, BS, BS), jnp.float32)
    summed, unused = lax.scan(one_shard, start_sum, jnp.arange(N_FRAME * N_CELL, dtype=jnp.int32))
    summed = summed.reshape(coarse_rows, 3, 3, N_CELL, BS, BS).transpose(0, 1, 2, 4, 3, 5)
    return summed.reshape(coarse_rows, 3, 3, BS, N_CELL * BS).astype(jnp.bfloat16)
```

```python
import functools

import jax
import jax.numpy as jnp
from jax import lax
from jax.experimental import pallas as pl
from jax.experimental.pallas import tpu as pltpu
from jax.sharding import PartitionSpec as P

AGG = 8
BS = 64


def shifted(value, axis):
    n = lax.axis_size(axis)
    up = [(i, i + 1) for i in range(n - 1)]
    down = [(i + 1, i) for i in range(n - 1)]
    return lax.ppermute(value, axis, up), lax.ppermute(value, axis, down)


def send_kernel(rows, nnz_a, meta, a_ref, pb, pm, pa, out, pall, apbuf, tbuf, count, psem, sems):
    copies = [
        pltpu.make_async_copy(src, pall.at[pl.ds(i * rows, rows)], psem.at[i])
        for i, src in enumerate((pb, pm, pa))
    ]
    for c in copies:
        c.start()

    def clear(i, _):
        count[i] = 0
        return 0

    lax.fori_loop(0, count.shape[0], clear, 0)
    for c in copies:
        c.wait()
    zero = jnp.zeros((BS, 2 * BS), jnp.bfloat16)

    def row(r, _):
        for m in range(nnz_a // 2):
            f0 = meta[r * 8 + 2 * m] & 63
            f1 = meta[r * 8 + 2 * m + 1] & 63
            rhs = jnp.concatenate(
                [
                    jnp.concatenate([pall[f0], zero], axis=1),
                    jnp.concatenate([zero, pall[f1]], axis=1),
                ],
                axis=0,
            )
            ap = jnp.dot(
                a_ref[r, :, 2 * BS * m : 2 * BS * (m + 1)], rhs, preferred_element_type=jnp.float32
            )
            apbuf[r, :, 4 * BS * m : 4 * BS * (m + 1)] = ap.astype(jnp.bfloat16)
        t = lax.dot_general(
            pall[rows + r], apbuf[r], (((0,), (0,)), ((), ())), preferred_element_type=jnp.float32
        )
        tbuf[r] = t.astype(jnp.bfloat16)
        for p in range(2):
            c = meta[r * 8 + 6 + p]
            place = count[c]
            count[c] = place + 1
            pltpu.make_async_copy(
                tbuf.at[r, pl.ds(p * BS, BS)],
                out.at[c, pl.ds(pl.multiple_of(place * BS, BS), BS)],
                sems.at[r * 2 + p],
            ).start()
        return 0

    lax.fori_loop(0, rows, row, 0, unroll=2)

    def finish(i, _):
        pltpu.make_async_copy(tbuf.at[0, pl.ds(0, BS)], out.at[0, pl.ds(0, BS)], sems.at[i]).wait()
        return 0

    lax.fori_loop(0, 2 * rows, finish, 0)


def add_kernel(nseg, cells, nnz_a, per, meta, slots, got, out, acc, stage, sems):
    i = pl.program_id(0)

    @pl.when(i == 0)
    def _():
        def clear(j, _):
            acc[pl.ds(j * 4, 4)] = jnp.zeros((4,) + acc.shape[1:], jnp.float32)
            return 0

        lax.fori_loop(0, acc.shape[0] // 4, clear, 0)

    low = lax.broadcasted_iota(jnp.int32, (BS, 2 * BS), 1) < BS

    def slot(j, _):
        s = i * per + j
        e = slots[s]

        @pl.when(e >= 0)
        def _():
            c = s // 2
            base = cells * 128 + c * 128 + (e // 2) * 8
            for k in range(nnz_a):
                w = meta[base + k]
                far = w & 63
                seg = w >> 6
                src = (far >> 4) * (cells * 128) + c * 128 + (far & 15) * 8 + 6
                i0 = seg * cells + meta[src]
                i1 = seg * cells + meta[src + 1]
                x = got[j, :, 2 * BS * k : 2 * BS * (k + 1)].astype(jnp.float32)
                new0 = acc[i0] + jnp.where(low, x, 0.0)
                new1 = acc[i1] + jnp.where(low, 0.0, x)
                acc[i0] = new0
                acc[i1] = new1

        return 0

    lax.fori_loop(0, per, slot, 0)

    @pl.when(i == pl.num_programs(0) - 1)
    def _():
        def put(seg, _):
            for h in range(cells // 2):
                a = acc[seg * cells + 2 * h]
                b = acc[seg * cells + 2 * h + 1]
                v = jnp.where(low, a, b) + pltpu.roll(jnp.where(low, b, a), BS, 1)
                stage[seg, :, 2 * BS * h : 2 * BS * (h + 1)] = v.astype(jnp.bfloat16)
            pltpu.make_async_copy(stage.at[seg], out.at[seg], sems.at[seg]).start()
            return 0

        lax.fori_loop(0, nseg, put, 0)

        def finish(seg, _):
            pltpu.make_async_copy(stage.at[seg], out.at[seg], sems.at[seg]).wait()
            return 0

        lax.fori_loop(0, nseg, finish, 0)


def local(a_blocks, a_cols, p_blocks, p_cells):
    rows = a_blocks.shape[0]
    nnz_a = a_cols.shape[1]
    cells = lax.axis_size("cell")
    frame = lax.axis_index("frame")
    me = lax.axis_index("cell")
    coarse_here = rows // AGG
    nseg = coarse_here * 9

    before, after = shifted(p_blocks, "frame")
    where_u = lax.div(a_cols, jnp.int32(rows * cells)) - frame + 1
    where_r = a_cols & (rows - 1)
    agg = jnp.arange(rows, dtype=jnp.int32)[:, None] // AGG
    seg = agg * 9 + where_u * 3 + where_r // AGG - agg + 1
    meta = jnp.concatenate([where_u * rows + where_r + 64 * seg, p_cells], axis=1).reshape(rows * 8)
    everyone = lax.all_to_all(
        jnp.broadcast_to(meta[None], (cells, rows * 8)), "cell", 0, 0, tiled=True
    )
    mb, ma = shifted(everyone, "frame")
    three = jnp.stack([mb, everyone, ma]).reshape(-1)
    named = everyone.reshape(cells, rows, 8)[:, :, 6:].reshape(cells, 2 * rows)
    entry = jnp.arange(2 * rows, dtype=jnp.int32)[None]
    hit = named == me
    first = jnp.min(jnp.where(hit, entry, 2 * rows), axis=1)
    last = jnp.max(jnp.where(hit, entry, -1), axis=1)
    slots = jnp.stack(
        [jnp.where(first < 2 * rows, first, -1), jnp.where(last > first, last, -1)], axis=1
    ).reshape(2 * cells)

    wide = 2 * nnz_a * BS
    any_spec = pl.BlockSpec(memory_space=pl.ANY)
    smem = pl.BlockSpec(memory_space=pltpu.SMEM)
    buffer = pl.pallas_call(
        functools.partial(send_kernel, rows, nnz_a),
        out_shape=jax.ShapeDtypeStruct((cells, 2 * BS, wide), jnp.bfloat16),
        in_specs=[smem, pl.BlockSpec(memory_space=pltpu.VMEM), any_spec, any_spec, any_spec],
        out_specs=any_spec,
        scratch_shapes=[
            pltpu.VMEM((3 * rows, BS, 2 * BS), jnp.bfloat16),
            pltpu.VMEM((rows, BS, wide), jnp.bfloat16),
            pltpu.VMEM((rows, 2 * BS, wide), jnp.bfloat16),
            pltpu.SMEM((cells,), jnp.int32),
            pltpu.SemaphoreType.DMA((3,)),
            pltpu.SemaphoreType.DMA((2 * rows,)),
        ],
        name="send",
    )(meta, a_blocks, before, p_blocks, after)
    got = lax.all_to_all(buffer, "cell", 0, 0, tiled=True).reshape(2 * cells, BS, wide)
    per = 8
    out = pl.pallas_call(
        functools.partial(add_kernel, nseg, cells, nnz_a, per),
        out_shape=jax.ShapeDtypeStruct((nseg, BS, cells * BS), jnp.bfloat16),
        grid=(2 * cells // per,),
        in_specs=[smem, smem, pl.BlockSpec((per, BS, wide), lambda i: (i, 0, 0))],
        out_specs=any_spec,
        scratch_shapes=[
            pltpu.VMEM((nseg * cells, BS, 2 * BS), jnp.float32),
            pltpu.VMEM((nseg, BS, cells * BS), jnp.bfloat16),
            pltpu.SemaphoreType.DMA((nseg,)),
        ],
        compiler_params=pltpu.CompilerParams(vmem_limit_bytes=50 << 20),
        name="add",
    )(three, slots, got)
    return out.reshape(coarse_here, 3, 3, BS, cells * BS)


def solution(mesh):
    placed = (
        P(("frame", "cell"), None, None),
        P(("frame", "cell"), None),
        P(("frame", "cell"), None, None),
        P(("frame", "cell"), None),
    )
    return jax.shard_map(
        local,
        mesh=mesh,
        in_specs=placed,
        out_specs=P(("frame", "cell"), None, None, None, None),
        check_vma=False,
    )
```

```python
import functools

import jax
import jax.numpy as jnp
from jax import lax
from jax.experimental import pallas as pl
from jax.experimental.pallas import tpu as pltpu
from jax.sharding import Mesh
from jax.sharding import PartitionSpec as P


AGG = 8
BS = 64
ANY = pl.BlockSpec(memory_space=pl.ANY)
SMEM = pl.BlockSpec(memory_space=pltpu.SMEM)


def shifted(value):
    n = lax.axis_size("frame")
    before = lax.ppermute(value, "frame", [(i, i + 1) for i in range(n - 1)])
    after = lax.ppermute(value, "frame", [(i + 1, i) for i in range(n - 1)])
    return before, after


def turned(up, down):
    n = lax.axis_size("z")
    up = lax.ppermute(up, "z", [(i, (i + 1) % n) for i in range(n)])
    if down is None:
        return (up,)
    down = lax.ppermute(down, "z", [((i + 1) % n, i) for i in range(n)])
    return up, down


def term_kernel(rows, nnz_a, nz, ny, offsets, pieces, first, meta, here, *refs):
    count = len(offsets)
    npieces = len(pieces)
    a_refs, p_refs = refs[:npieces], refs[npieces : npieces + count]
    before, after, out, abuf, pall, apbuf, obuf, placed, listed, sems = refs[npieces + count :]
    copies = []

    def fetch(src, dst):
        copy = pltpu.make_async_copy(src, dst, sems.at[len(copies)])
        copy.start()
        copies.append(copy)

    for (s, start, size), a_ref in zip(pieces, a_refs):
        fetch(a_ref, abuf.at[s, pl.ds(start, size)])
    for s, p_ref in enumerate(p_refs[:count]):
        fetch(p_ref, pall.at[s, pl.ds(rows, rows)])
        fetch(before.at[pl.ds((first + s) * rows, rows)], pall.at[s, pl.ds(0, rows)])
        fetch(after.at[pl.ds((first + s) * rows, rows)], pall.at[s, pl.ds(2 * rows, rows)])
    z, y = here[0], here[1]
    bases, active = [], []
    for s, offset in enumerate(offsets):
        base = (lax.rem(z + offset + nz, nz) * ny + y) * 128
        bases.append(base)
        for i in range(ny):
            placed[s * ny + i] = 0
        listed[s * (rows + 1)] = 0

        def look(r, n, s=s, base=base):
            z0 = meta[base + r * 8 + 6] // ny
            z1 = meta[base + r * 8 + 7] // ny
            listed[s * (rows + 1) + n] = r
            return n + jnp.where((z0 == z) | (z1 == z), 1, 0)

        active.append(lax.fori_loop(0, rows, look, 0))
    for copy in copies:
        copy.wait()
    zero = jnp.zeros((BS, 2 * BS), jnp.bfloat16)
    trash = ny * 2 * count

    def row(i, _):
        picked = []
        for s in range(count):
            live = i < active[s]
            r = listed[s * (rows + 1) + jnp.where(live, i, 0)]
            base = bases[s] + r * 8
            picked.append((live, r, base))
            for m in range(nnz_a // 2):
                f0 = meta[base + 2 * m] & 63
                f1 = meta[base + 2 * m + 1] & 63
                rhs = jnp.concatenate(
                    [
                        jnp.concatenate([pall[s, f0], zero], axis=1),
                        jnp.concatenate([zero, pall[s, f1]], axis=1),
                    ],
                    axis=0,
                )
                ap = jnp.dot(
                    abuf[s, r, :, 2 * BS * m : 2 * BS * (m + 1)],
                    rhs,
                    preferred_element_type=jnp.float32,
                )
                apbuf[s, :, 4 * BS * m : 4 * BS * (m + 1)] = ap.astype(jnp.bfloat16)
        for s in range(count):
            live, r, base = picked[s]
            t = lax.dot_general(
                pall[s, rows + r],
                apbuf[s],
                (((0,), (0,)), ((), ())),
                preferred_element_type=jnp.float32,
            ).astype(jnp.bfloat16)
            for p in range(2):
                c = meta[base + 6 + p] - z * ny
                fits = live & (c >= 0) & (c < ny)
                c = jnp.where(fits, c, 0)
                place = placed[s * ny + c]
                placed[s * ny + c] = place + jnp.where(fits, 1, 0)
                slot = jnp.where(fits, c * (2 * count) + 2 * s + place, trash)
                obuf[slot] = t[p * BS : (p + 1) * BS]
        return 0

    most = active[0]
    for n in active[1:]:
        most = jnp.maximum(most, n)
    lax.fori_loop(0, most, row, 0)
    copy = pltpu.make_async_copy(obuf.at[pl.ds(0, trash)], out, sems.at[0])
    copy.start()
    copy.wait()


def add_kernel(nseg, nz, ny, nnz_a, offsets, meta, slots, here, *refs):
    chunks = len(offsets)
    got, out, bufs = refs[:chunks], refs[chunks], refs[chunks + 1 : 2 * chunks + 1]
    acc, stage, insems, sems = refs[2 * chunks + 1 :]
    cells = nz * ny
    for i in range(chunks):
        pltpu.make_async_copy(got[i], bufs[i], insems.at[i]).start()

    def clear(j, _):
        acc[pl.ds(j * 4, 4)] = jnp.zeros((4,) + acc.shape[1:], jnp.float32)
        return 0

    lax.fori_loop(0, acc.shape[0] // 4, clear, 0)
    low = lax.broadcasted_iota(jnp.int32, (BS, 2 * BS), 1) < BS
    z = here[0]
    for i in range(chunks):
        pltpu.make_async_copy(got[i], bufs[i], insems.at[i]).wait()
        for s, offset in enumerate(offsets[i]):
            zs = lax.rem(z + offset + nz, nz)

            def slot(j, _, i=i, s=s, zs=zs):
                y = j // 2
                c = zs * ny + y
                e = slots[2 * c + (j & 1)]

                @pl.when(e >= 0)
                def _():
                    base = cells * 128 + c * 128 + (e // 2) * 8
                    for k in range(nnz_a):
                        w = meta[base + k]
                        far = w & 63
                        seg = w >> 6
                        src = (far >> 4) * (cells * 128) + c * 128 + (far & 15) * 8 + 6
                        i0 = seg * cells + meta[src]
                        i1 = seg * cells + meta[src + 1]
                        x = bufs[i][y, 2 * s + (j & 1), :, 2 * BS * k : 2 * BS * (k + 1)]
                        x = x.astype(jnp.float32)
                        new0 = acc[i0] + jnp.where(low, x, 0.0)
                        new1 = acc[i1] + jnp.where(low, 0.0, x)
                        acc[i0] = new0
                        acc[i1] = new1

                return 0

            lax.fori_loop(0, 2 * ny, slot, 0)

    def put(seg, _):
        for h in range(cells // 2):
            a = acc[seg * cells + 2 * h]
            b = acc[seg * cells + 2 * h + 1]
            v = jnp.where(low, a, b) + pltpu.roll(jnp.where(low, b, a), BS, 1)
            stage[seg, :, 2 * BS * h : 2 * BS * (h + 1)] = v.astype(jnp.bfloat16)
        pltpu.make_async_copy(stage.at[seg], out.at[seg], sems.at[seg]).start()
        return 0

    lax.fori_loop(0, nseg, put, 0)

    def finish(seg, _):
        pltpu.make_async_copy(stage.at[seg], out.at[seg], sems.at[seg]).wait()
        return 0

    lax.fori_loop(0, nseg, finish, 0)


def last_kernel(nz, ny, nnz_a, offset, meta, slots, here, part, got, out, buf, stage, sems):
    cells = nz * ny
    loads = [
        pltpu.make_async_copy(part, stage, sems.at[0]),
        pltpu.make_async_copy(got, buf, sems.at[1]),
    ]
    for copy in loads:
        copy.start()
    for copy in loads:
        copy.wait()
    upper = lax.broadcasted_iota(jnp.int32, (BS, 2 * BS), 1) // BS
    zs = lax.rem(here[0] + offset + nz, nz)

    def slot(j, _):
        y = j // 2
        c = zs * ny + y
        e = slots[2 * c + (j & 1)]

        @pl.when(e >= 0)
        def _():
            base = cells * 128 + c * 128 + (e // 2) * 8
            for k in range(nnz_a):
                w = meta[base + k]
                far = w & 63
                seg = w >> 6
                src = (far >> 4) * (cells * 128) + c * 128 + (far & 15) * 8 + 6
                x = buf[y, j & 1, :, 2 * BS * k : 2 * BS * (k + 1)].astype(jnp.float32)
                turned_x = pltpu.roll(x, BS, 1)
                for q in range(2):
                    cell = meta[src + q]
                    side = cell & 1
                    lanes = pl.ds(pl.multiple_of((cell >> 1) * (2 * BS), 2 * BS), 2 * BS)
                    v = jnp.where(upper == side, jnp.where(side == q, x, turned_x), 0.0)
                    old = stage[seg, :, lanes].astype(jnp.float32)
                    stage[seg, :, lanes] = (old + v).astype(jnp.bfloat16)

        return 0

    lax.fori_loop(0, 2 * ny, slot, 0)
    copy = pltpu.make_async_copy(stage, out, sems.at[2])
    copy.start()
    copy.wait()


def local(a_blocks, a_cols, p_blocks, p_cells):
    rows = a_blocks.shape[0]
    nnz_a = a_cols.shape[1]
    nz, ny = lax.axis_size("z"), lax.axis_size("y")
    cells = nz * ny
    frame, z, y = lax.axis_index("frame"), lax.axis_index("z"), lax.axis_index("y")
    coarse_here = rows // AGG
    nseg = coarse_here * 9
    half = nz // 2
    mid = rows // 2
    wide = 2 * nnz_a * BS

    p_ring, a_ring = [(p_blocks, p_blocks)], [(a_blocks, a_blocks)]
    for d in range(1, half + 1):
        up, down = p_ring[-1]
        p_ring.append(turned(up, None if d == half else down))
        up, down = a_ring[-1]
        if d == half:
            up, down = up[:mid], down[mid:]
        a_ring.append(turned(up, down))

    where_u = lax.div(a_cols, jnp.int32(rows * cells)) - frame + 1
    where_r = a_cols & (rows - 1)
    agg = jnp.arange(rows, dtype=jnp.int32)[:, None] // AGG
    seg = agg * 9 + where_u * 3 + where_r // AGG - agg + 1
    meta = jnp.concatenate([where_u * rows + where_r + 64 * seg, p_cells], axis=1).reshape(rows * 8)
    everyone = lax.all_to_all(
        jnp.broadcast_to(meta[None], (cells, rows * 8)), ("z", "y"), 0, 0, tiled=True
    )
    mb, ma = shifted(everyone)
    three = jnp.stack([mb, everyone, ma]).reshape(-1)
    flat = everyone.reshape(-1)
    named = everyone.reshape(cells, rows, 8)[:, :, 6:].reshape(cells, 2 * rows)
    entry = jnp.arange(2 * rows, dtype=jnp.int32)[None]
    hit = named == z * ny + y
    first = jnp.min(jnp.where(hit, entry, 2 * rows), axis=1)
    last = jnp.max(jnp.where(hit, entry, -1), axis=1)
    slots = jnp.stack(
        [jnp.where(first < 2 * rows, first, -1), jnp.where(last > first, last, -1)], axis=1
    ).reshape(2 * cells)
    here = jnp.stack([z, y]).astype(jnp.int32)

    whole = (0, rows)
    whole = (0, rows)
    three_rings = zip((p_blocks,) + p_ring[1], (a_blocks,) + a_ring[1])
    p_list, a_list = zip(*three_rings)
    groups = [((0, -1, 1), tuple((i, *whole) for i in range(3)), a_list, p_list, 0, 0)]
    for d in range(2, half):
        groups.append(((-d, d), ((0, *whole), (1, *whole)), a_ring[d], p_ring[d], d - 1, 0))
    groups.append(((half,), ((0, 0, mid), (0, mid, mid)), a_ring[half], p_ring[half], 2, 2))
    batches = [
        (p_blocks,) + p_ring[1],
        p_ring[2],
        p_ring[3] + p_ring[4],
    ]
    near = {}
    got = []
    for i, (offsets, pieces, a_list, p_list, batch, start) in enumerate(groups):
        if batch not in near:
            parts = batches[batch]
            if i == 2:
                *parts, sent = lax.optimization_barrier((*parts, sent))
            near[batch] = shifted(jnp.concatenate(parts, axis=0))
        if i > 0:
            if i > 1:
                sent, got[-1] = lax.optimization_barrier((sent, got[-1]))
            got.append(lax.all_to_all(sent, "y", 0, 0, tiled=True))
        pb, pa = near[batch]
        count = len(offsets)
        sent = pl.pallas_call(
            functools.partial(term_kernel, rows, nnz_a, nz, ny, offsets, pieces, start),
            out_shape=jax.ShapeDtypeStruct((ny * 2 * count, BS, wide), jnp.bfloat16),
            in_specs=[SMEM, SMEM] + [ANY] * (len(a_list) + len(p_list) + 2),
            out_specs=ANY,
            scratch_shapes=[
                pltpu.VMEM((count, rows, BS, nnz_a * BS), jnp.bfloat16),
                pltpu.VMEM((count, 3 * rows, BS, 2 * BS), jnp.bfloat16),
                pltpu.VMEM((count, BS, wide), jnp.bfloat16),
                pltpu.VMEM((ny * 2 * count + 1, BS, wide), jnp.bfloat16),
                pltpu.SMEM((count * ny,), jnp.int32),
                pltpu.SMEM((count * (rows + 1),), jnp.int32),
                pltpu.SemaphoreType.DMA((len(pieces) + 3 * count,)),
            ],
            compiler_params=pltpu.CompilerParams(vmem_limit_bytes=24 << 20),
            name="terms",
        )(flat, here, *a_list, *p_list, pb, pa)
        sent = sent.reshape(ny, 2 * count, BS, wide)
    sent, got[-1] = lax.optimization_barrier((sent, got[-1]))
    got.append(lax.all_to_all(sent, "y", 0, 0, tiled=True))
    offsets = [g[0] for g in groups]
    result = jax.ShapeDtypeStruct((nseg, BS, cells * BS), jnp.bfloat16)
    early = got[:-1]
    part = pl.pallas_call(
        functools.partial(add_kernel, nseg, nz, ny, nnz_a, offsets[:-1]),
        out_shape=result,
        in_specs=[SMEM, SMEM, SMEM] + [ANY] * len(early),
        out_specs=ANY,
        scratch_shapes=[pltpu.VMEM(g.shape, g.dtype) for g in early]
        + [
            pltpu.VMEM((nseg * cells, BS, 2 * BS), jnp.float32),
            pltpu.VMEM(result.shape, result.dtype),
            pltpu.SemaphoreType.DMA((len(early),)),
            pltpu.SemaphoreType.DMA((nseg,)),
        ],
        compiler_params=pltpu.CompilerParams(vmem_limit_bytes=60 << 20),
        name="add",
    )(three, slots, here, *early)
    out = pl.pallas_call(
        functools.partial(last_kernel, nz, ny, nnz_a, half),
        out_shape=result,
        in_specs=[SMEM, SMEM, SMEM, ANY, ANY],
        out_specs=ANY,
        scratch_shapes=[
            pltpu.VMEM(got[-1].shape, jnp.bfloat16),
            pltpu.VMEM(result.shape, result.dtype),
            pltpu.SemaphoreType.DMA((3,)),
        ],
        compiler_params=pltpu.CompilerParams(vmem_limit_bytes=60 << 20),
        name="finish",
    )(three, slots, here, part, got[-1])
    return out.reshape(coarse_here, 3, 3, BS, cells * BS)


def solution(mesh):
    frames = mesh.shape["frame"]
    grid = Mesh(mesh.devices.reshape(frames, 8, -1), ("frame", "z", "y"))
    dim = ("frame", "z", "y")

    return jax.shard_map(
        local,
        mesh=grid,
        in_specs=(P(dim, None, None), P(dim, None), P(dim, None, None), P(dim, None)),
        out_specs=P(dim, None, None, None, None),
        check_vma=False,
    )
```

```python
import functools

import jax
import jax.numpy as jnp
from jax import lax
from jax.experimental import pallas as pl
from jax.experimental.pallas import tpu as pltpu
from jax.sharding import Mesh
from jax.sharding import PartitionSpec as P


AGG = 8
BS = 64
ANY = pl.BlockSpec(memory_space=pl.ANY)
SMEM = pl.BlockSpec(memory_space=pltpu.SMEM)


def shifted(value):
    n = lax.axis_size("frame")
    before = lax.ppermute(value, "frame", [(i, i + 1) for i in range(n - 1)])
    after = lax.ppermute(value, "frame", [(i + 1, i) for i in range(n - 1)])
    return before, after


def turned(up, down):
    n = lax.axis_size("z")
    up = lax.ppermute(up, "z", [(i, (i + 1) % n) for i in range(n)])
    if down is None:
        return (up,)
    down = lax.ppermute(down, "z", [((i + 1) % n, i) for i in range(n)])
    return up, down


def term_kernel(rows, nnz_a, nz, ny, offsets, pieces, first, apart, meta, here, *refs):
    count = len(offsets)
    npieces = len(pieces)
    a_refs, p_refs = refs[:npieces], refs[npieces : npieces + count]
    before, after = refs[npieces + count : npieces + count + 2]
    outs = refs[npieces + count + 2 : -7]
    abuf, pall, apbuf, obuf, placed, listed, sems = refs[-7:]
    copies = []

    def fetch(src, dst):
        copy = pltpu.make_async_copy(src, dst, sems.at[len(copies)])
        copy.start()
        copies.append(copy)

    for (s, start, size), a_ref in zip(pieces, a_refs):
        fetch(a_ref, abuf.at[s, pl.ds(start, size)])
    for s, p_ref in enumerate(p_refs[:count]):
        fetch(p_ref, pall.at[s, pl.ds(rows, rows)])
        fetch(before.at[pl.ds((first + s) * rows, rows)], pall.at[s, pl.ds(0, rows)])
        fetch(after.at[pl.ds((first + s) * rows, rows)], pall.at[s, pl.ds(2 * rows, rows)])
    z, y = here[0], here[1]
    bases, active = [], []
    for s, offset in enumerate(offsets):
        base = (lax.rem(z + offset + nz, nz) * ny + y) * 128
        bases.append(base)
        for i in range(ny):
            placed[s * ny + i] = 0
        listed[s * (rows + 1)] = 0

        def look(r, n, s=s, base=base):
            z0 = meta[base + r * 8 + 6] // ny
            z1 = meta[base + r * 8 + 7] // ny
            listed[s * (rows + 1) + n] = r
            return n + jnp.where((z0 == z) | (z1 == z), 1, 0)

        active.append(lax.fori_loop(0, rows, look, 0))
    for copy in copies:
        copy.wait()
    zero = jnp.zeros((BS, 2 * BS), jnp.bfloat16)
    trash = ny * 2 * count

    def row(i, _):
        picked = []
        for s in range(count):
            live = i < active[s]
            r = listed[s * (rows + 1) + jnp.where(live, i, 0)]
            base = bases[s] + r * 8
            picked.append((live, r, base))
            for m in range(nnz_a // 2):
                f0 = meta[base + 2 * m] & 63
                f1 = meta[base + 2 * m + 1] & 63
                rhs = jnp.concatenate(
                    [
                        jnp.concatenate([pall[s, f0], zero], axis=1),
                        jnp.concatenate([zero, pall[s, f1]], axis=1),
                    ],
                    axis=0,
                )
                ap = jnp.dot(
                    abuf[s, r, :, 2 * BS * m : 2 * BS * (m + 1)],
                    rhs,
                    preferred_element_type=jnp.float32,
                )
                apbuf[s, :, 4 * BS * m : 4 * BS * (m + 1)] = ap.astype(jnp.bfloat16)
        for s in range(count):
            live, r, base = picked[s]
            t = lax.dot_general(
                pall[s, rows + r],
                apbuf[s],
                (((0,), (0,)), ((), ())),
                preferred_element_type=jnp.float32,
            ).astype(jnp.bfloat16)
            for p in range(2):
                c = meta[base + 6 + p] - z * ny
                fits = live & (c >= 0) & (c < ny)
                c = jnp.where(fits, c, 0)
                place = placed[s * ny + c]
                placed[s * ny + c] = place + jnp.where(fits, 1, 0)
                to = lax.rem(c - y + ny, ny) if apart else c
                slot = jnp.where(fits, to * (2 * count) + 2 * s + place, trash)
                obuf[slot] = t[p * BS : (p + 1) * BS]
        return 0

    most = active[0]
    for n in active[1:]:
        most = jnp.maximum(most, n)
    lax.fori_loop(0, most, row, 0)
    size = trash // len(outs)
    copies = [
        pltpu.make_async_copy(obuf.at[pl.ds(i * size, size)], out, sems.at[i])
        for i, out in enumerate(outs)
    ]
    for copy in copies:
        copy.start()
    for copy in copies:
        copy.wait()


def add_kernel(nseg, nz, ny, nnz_a, offsets, meta, slots, here, *refs):
    chunks = len(offsets)
    got, out, bufs = refs[:chunks], refs[chunks], refs[chunks + 1 : 2 * chunks + 1]
    acc, stage, insems, sems = refs[2 * chunks + 1 :]
    cells = nz * ny
    for i in range(chunks):
        pltpu.make_async_copy(got[i], bufs[i], insems.at[i]).start()

    def clear(j, _):
        acc[pl.ds(j * 4, 4)] = jnp.zeros((4,) + acc.shape[1:], jnp.float32)
        return 0

    lax.fori_loop(0, acc.shape[0] // 4, clear, 0)
    low = lax.broadcasted_iota(jnp.int32, (BS, 2 * BS), 1) < BS
    z = here[0]
    for i in range(chunks):
        pltpu.make_async_copy(got[i], bufs[i], insems.at[i]).wait()
        for s, offset in enumerate(offsets[i]):
            zs = lax.rem(z + offset + nz, nz)

            def slot(j, _, i=i, s=s, zs=zs):
                y = j // 2
                c = zs * ny + y
                e = slots[2 * c + (j & 1)]

                @pl.when(e >= 0)
                def _():
                    base = cells * 128 + c * 128 + (e // 2) * 8
                    for k in range(nnz_a):
                        w = meta[base + k]
                        far = w & 63
                        seg = w >> 6
                        src = (far >> 4) * (cells * 128) + c * 128 + (far & 15) * 8 + 6
                        i0 = seg * cells + meta[src]
                        i1 = seg * cells + meta[src + 1]
                        x = bufs[i][y, 2 * s + (j & 1), :, 2 * BS * k : 2 * BS * (k + 1)]
                        x = x.astype(jnp.float32)
                        new0 = acc[i0] + jnp.where(low, x, 0.0)
                        new1 = acc[i1] + jnp.where(low, 0.0, x)
                        acc[i0] = new0
                        acc[i1] = new1

                return 0

            lax.fori_loop(0, 2 * ny, slot, 0)

    def put(seg, _):
        for h in range(cells // 2):
            a = acc[seg * cells + 2 * h]
            b = acc[seg * cells + 2 * h + 1]
            v = jnp.where(low, a, b) + pltpu.roll(jnp.where(low, b, a), BS, 1)
            stage[seg, :, 2 * BS * h : 2 * BS * (h + 1)] = v
        pltpu.make_async_copy(stage.at[seg], out.at[seg], sems.at[seg]).start()
        return 0

    lax.fori_loop(0, nseg, put, 0)

    def finish(seg, _):
        pltpu.make_async_copy(stage.at[seg], out.at[seg], sems.at[seg]).wait()
        return 0

    lax.fori_loop(0, nseg, finish, 0)


def last_kernel(nseg, nz, ny, nnz_a, offsets, offset, meta, slots, here, part, got, *refs):
    apart, out, acc, buf, late, stage, loadsems, sems = refs[:ny], *refs[ny:]
    cells = nz * ny
    loads = [pltpu.make_async_copy(part, acc, loadsems.at[0])]
    loads.append(pltpu.make_async_copy(got, buf, loadsems.at[1]))
    for i in range(ny):
        loads.append(pltpu.make_async_copy(apart[i], late.at[i], loadsems.at[2 + i]))
    for copy in loads:
        copy.start()
    for copy in loads:
        copy.wait()
    upper = lax.broadcasted_iota(jnp.int32, (BS, 2 * BS), 1) // BS
    z, y = here[0], here[1]

    def add(c, which, load):
        e = slots[2 * c + which]

        @pl.when(e >= 0)
        def _():
            base = cells * 128 + c * 128 + (e // 2) * 8
            for k in range(nnz_a):
                w = meta[base + k]
                far = w & 63
                seg = w >> 6
                src = (far >> 4) * (cells * 128) + c * 128 + (far & 15) * 8 + 6
                x = load(slice(2 * BS * k, 2 * BS * (k + 1))).astype(jnp.float32)
                turned_x = pltpu.roll(x, BS, 1)
                for q in range(2):
                    cell = meta[src + q]
                    side = cell & 1
                    lanes = pl.ds(pl.multiple_of((cell >> 1) * (2 * BS), 2 * BS), 2 * BS)
                    v = jnp.where(upper == side, jnp.where(side == q, x, turned_x), 0.0)
                    acc[seg, :, lanes] = acc[seg, :, lanes] + v

    for s, near in enumerate(offsets):
        zs = lax.rem(z + near + nz, nz)

        def slot(j, _, s=s, zs=zs):
            add(zs * ny + j // 2, j & 1, lambda cols: buf[j // 2, 2 * s + (j & 1), :, cols])
            return 0

        lax.fori_loop(0, 2 * ny, slot, 0)
    zs = lax.rem(z + offset + nz, nz)

    def slot(j, _):
        ys = lax.rem(y - j // 2 + ny, ny)
        add(zs * ny + ys, j & 1, lambda cols: late[j // 2, j & 1, :, cols])
        return 0

    lax.fori_loop(0, 2 * ny, slot, 0)

    def put(seg, _):
        stage[seg] = acc[seg].astype(jnp.bfloat16)
        pltpu.make_async_copy(stage.at[seg], out.at[seg], sems.at[seg]).start()
        return 0

    lax.fori_loop(0, nseg, put, 0)

    def finish(seg, _):
        pltpu.make_async_copy(stage.at[seg], out.at[seg], sems.at[seg]).wait()
        return 0

    lax.fori_loop(0, nseg, finish, 0)


def local(a_blocks, a_cols, p_blocks, p_cells):
    rows = a_blocks.shape[0]
    nnz_a = a_cols.shape[1]
    nz, ny = lax.axis_size("z"), lax.axis_size("y")
    cells = nz * ny
    frame, z, y = lax.axis_index("frame"), lax.axis_index("z"), lax.axis_index("y")
    coarse_here = rows // AGG
    nseg = coarse_here * 9
    half = nz // 2
    mid = rows // 2
    wide = 2 * nnz_a * BS

    p_ring, a_ring = [(p_blocks, p_blocks)], [(a_blocks, a_blocks)]
    for d in range(1, half + 1):
        up, down = p_ring[-1]
        p_ring.append(turned(up, None if d == half else down))
        up, down = a_ring[-1]
        if d == half:
            up, down = up[:mid], down[mid:]
        a_ring.append(turned(up, down))

    where_u = lax.div(a_cols, jnp.int32(rows * cells)) - frame + 1
    where_r = a_cols & (rows - 1)
    agg = jnp.arange(rows, dtype=jnp.int32)[:, None] // AGG
    seg = agg * 9 + where_u * 3 + where_r // AGG - agg + 1
    meta = jnp.concatenate([where_u * rows + where_r + 64 * seg, p_cells], axis=1).reshape(rows * 8)
    everyone = lax.all_to_all(
        jnp.broadcast_to(meta[None], (cells, rows * 8)), ("z", "y"), 0, 0, tiled=True
    )
    mb, ma = shifted(everyone)
    three = jnp.stack([mb, everyone, ma]).reshape(-1)
    flat = everyone.reshape(-1)
    named = everyone.reshape(cells, rows, 8)[:, :, 6:].reshape(cells, 2 * rows)
    entry = jnp.arange(2 * rows, dtype=jnp.int32)[None]
    hit = named == z * ny + y
    first = jnp.min(jnp.where(hit, entry, 2 * rows), axis=1)
    last = jnp.max(jnp.where(hit, entry, -1), axis=1)
    slots = jnp.stack(
        [jnp.where(first < 2 * rows, first, -1), jnp.where(last > first, last, -1)], axis=1
    ).reshape(2 * cells)
    here = jnp.stack([z, y]).astype(jnp.int32)

    whole = (0, rows)
    whole = (0, rows)
    three_rings = zip((p_blocks,) + p_ring[1], (a_blocks,) + a_ring[1])
    p_list, a_list = zip(*three_rings)
    groups = [((0, -1, 1), tuple((i, *whole) for i in range(3)), a_list, p_list, 0, 0)]
    for d in range(2, half):
        groups.append(((-d, d), ((0, *whole), (1, *whole)), a_ring[d], p_ring[d], d - 1, 0))
    groups.append(((half,), ((0, 0, mid), (0, mid, mid)), a_ring[half], p_ring[half], 2, 2))
    batches = [
        (p_blocks,) + p_ring[1],
        p_ring[2],
        p_ring[3] + p_ring[4],
    ]
    near = {}
    got = []
    for i, (offsets, pieces, a_list, p_list, batch, start) in enumerate(groups):
        if batch not in near:
            parts = batches[batch]
            if i == 2:
                *parts, sent = lax.optimization_barrier((*parts, sent))
            near[batch] = shifted(jnp.concatenate(parts, axis=0))
        if i > 0:
            if i > 1:
                sent, got[-1] = lax.optimization_barrier((sent, got[-1]))
            got.append(lax.all_to_all(sent, "y", 0, 0, tiled=True))
        pb, pa = near[batch]
        count = len(offsets)
        apart = i == len(groups) - 1
        parts_out = ny if apart else 1
        shape = (ny * 2 * count // parts_out, BS, wide)
        sent = pl.pallas_call(
            functools.partial(
                term_kernel, rows, nnz_a, nz, ny, offsets, pieces, start, apart
            ),
            out_shape=[jax.ShapeDtypeStruct(shape, jnp.bfloat16)] * parts_out,
            in_specs=[SMEM, SMEM] + [ANY] * (len(a_list) + len(p_list) + 2),
            out_specs=[ANY] * parts_out,
            scratch_shapes=[
                pltpu.VMEM((count, rows, BS, nnz_a * BS), jnp.bfloat16),
                pltpu.VMEM((count, 3 * rows, BS, 2 * BS), jnp.bfloat16),
                pltpu.VMEM((count, BS, wide), jnp.bfloat16),
                pltpu.VMEM((ny * 2 * count + 1, BS, wide), jnp.bfloat16),
                pltpu.SMEM((count * ny,), jnp.int32),
                pltpu.SMEM((count * (rows + 1),), jnp.int32),
                pltpu.SemaphoreType.DMA((len(pieces) + 3 * count + ny,)),
            ],
            compiler_params=pltpu.CompilerParams(vmem_limit_bytes=24 << 20),
            name="terms",
        )(flat, here, *a_list, *p_list, pb, pa)
        if apart:
            break
        sent = sent[0].reshape(ny, 2 * count, BS, wide)
    late = [sent[0]]
    for by in (1, 2, ny - 1):
        late.append(lax.ppermute(sent[by], "y", [(i, (i + by) % ny) for i in range(ny)]))
    offsets = [g[0] for g in groups]
    shape = (nseg, BS, cells * BS)
    early = got[:-1]
    part = pl.pallas_call(
        functools.partial(add_kernel, nseg, nz, ny, nnz_a, offsets[:-2]),
        out_shape=jax.ShapeDtypeStruct(shape, jnp.float32),
        in_specs=[SMEM, SMEM, SMEM] + [ANY] * len(early),
        out_specs=ANY,
        scratch_shapes=[pltpu.VMEM(g.shape, g.dtype) for g in early]
        + [
            pltpu.VMEM((nseg * cells, BS, 2 * BS), jnp.float32),
            pltpu.VMEM(shape, jnp.float32),
            pltpu.SemaphoreType.DMA((len(early),)),
            pltpu.SemaphoreType.DMA((nseg,)),
        ],
        compiler_params=pltpu.CompilerParams(vmem_limit_bytes=60 << 20),
        name="add",
    )(three, slots, here, *early)
    out = pl.pallas_call(
        functools.partial(last_kernel, nseg, nz, ny, nnz_a, offsets[-2], half),
        out_shape=jax.ShapeDtypeStruct(shape, jnp.bfloat16),
        in_specs=[SMEM, SMEM, SMEM] + [ANY] * (2 + ny),
        out_specs=ANY,
        scratch_shapes=[
            pltpu.VMEM(shape, jnp.float32),
            pltpu.VMEM(got[-1].shape, jnp.bfloat16),
            pltpu.VMEM((ny, 2, BS, wide), jnp.bfloat16),
            pltpu.VMEM(shape, jnp.bfloat16),
            pltpu.SemaphoreType.DMA((2 + ny,)),
            pltpu.SemaphoreType.DMA((nseg,)),
        ],
        compiler_params=pltpu.CompilerParams(vmem_limit_bytes=60 << 20),
        name="finish",
    )(three, slots, here, part, got[-1], *late)
    return out.reshape(coarse_here, 3, 3, BS, cells * BS)


def solution(mesh):
    frames = mesh.shape["frame"]
    grid = Mesh(mesh.devices.reshape(frames, 8, -1), ("frame", "z", "y"))
    dim = ("frame", "z", "y")

    return jax.shard_map(
        local,
        mesh=grid,
        in_specs=(P(dim, None, None), P(dim, None), P(dim, None, None), P(dim, None)),
        out_specs=P(dim, None, None, None, None),
        check_vma=False,
    )
```

```python
import functools

import jax
import jax.numpy as jnp
from jax import lax
from jax.experimental import pallas as pl
from jax.experimental.pallas import tpu as pltpu
from jax.sharding import Mesh
from jax.sharding import PartitionSpec as P


AGG = 8
BS = 64
ANY = pl.BlockSpec(memory_space=pl.ANY)
SMEM = pl.BlockSpec(memory_space=pltpu.SMEM)


def shifted(value):
    n = lax.axis_size("frame")
    before = lax.ppermute(value, "frame", [(i, i + 1) for i in range(n - 1)])
    after = lax.ppermute(value, "frame", [(i + 1, i) for i in range(n - 1)])
    return before, after


def turned(up, down):
    n = lax.axis_size("z")
    up = lax.ppermute(up, "z", [(i, (i + 1) % n) for i in range(n)])
    if down is None:
        return (up,)
    down = lax.ppermute(down, "z", [((i + 1) % n, i) for i in range(n)])
    return up, down


def term_kernel(rows, nnz_a, nz, ny, offsets, pieces, first, apart, meta, here, *refs):
    count = len(offsets)
    npieces = len(pieces)
    a_refs, p_refs = refs[:npieces], refs[npieces : npieces + count]
    before, after = refs[npieces + count : npieces + count + 2]
    outs = refs[npieces + count + 2 : -7]
    abuf, pall, apbuf, obuf, placed, listed, sems = refs[-7:]
    copies = []

    def fetch(src, dst):
        copy = pltpu.make_async_copy(src, dst, sems.at[len(copies)])
        copy.start()
        copies.append(copy)

    for (s, start, size), a_ref in zip(pieces, a_refs):
        fetch(a_ref, abuf.at[s, pl.ds(start, size)])
    for s, p_ref in enumerate(p_refs[:count]):
        fetch(p_ref, pall.at[s, pl.ds(rows, rows)])
        fetch(before.at[pl.ds((first + s) * rows, rows)], pall.at[s, pl.ds(0, rows)])
        fetch(after.at[pl.ds((first + s) * rows, rows)], pall.at[s, pl.ds(2 * rows, rows)])
    z, y = here[0], here[1]
    bases, active = [], []
    for s, offset in enumerate(offsets):
        base = (lax.rem(z + offset + nz, nz) * ny + y) * 128
        bases.append(base)
        for i in range(ny):
            placed[s * ny + i] = 0
        listed[s * (rows + 1)] = 0

        def look(r, n, s=s, base=base):
            z0 = meta[base + r * 8 + 6] // ny
            z1 = meta[base + r * 8 + 7] // ny
            listed[s * (rows + 1) + n] = r
            return n + jnp.where((z0 == z) | (z1 == z), 1, 0)

        active.append(lax.fori_loop(0, rows, look, 0))
    for copy in copies:
        copy.wait()
    zero = jnp.zeros((BS, 2 * BS), jnp.bfloat16)
    trash = ny * 2 * count

    def row(i, _):
        picked = []
        for s in range(count):
            live = i < active[s]
            r = listed[s * (rows + 1) + jnp.where(live, i, 0)]
            base = bases[s] + r * 8
            picked.append((live, r, base))
            for m in range(nnz_a // 2):
                f0 = meta[base + 2 * m] & 63
                f1 = meta[base + 2 * m + 1] & 63
                rhs = jnp.concatenate(
                    [
                        jnp.concatenate([pall[s, f0], zero], axis=1),
                        jnp.concatenate([zero, pall[s, f1]], axis=1),
                    ],
                    axis=0,
                )
                ap = jnp.dot(
                    abuf[s, r, :, 2 * BS * m : 2 * BS * (m + 1)],
                    rhs,
                    preferred_element_type=jnp.float32,
                )
                apbuf[s, :, 4 * BS * m : 4 * BS * (m + 1)] = ap.astype(jnp.bfloat16)
        for s in range(count):
            live, r, base = picked[s]
            t = lax.dot_general(
                pall[s, rows + r],
                apbuf[s],
                (((0,), (0,)), ((), ())),
                preferred_element_type=jnp.float32,
            ).astype(jnp.bfloat16)
            for p in range(2):
                c = meta[base + 6 + p] - z * ny
                fits = live & (c >= 0) & (c < ny)
                c = jnp.where(fits, c, 0)
                place = placed[s * ny + c]
                placed[s * ny + c] = place + jnp.where(fits, 1, 0)
                to = lax.rem(c - y + ny, ny) if apart else c
                slot = jnp.where(fits, to * (2 * count) + 2 * s + place, trash)
                obuf[slot] = t[p * BS : (p + 1) * BS]
        return 0

    most = active[0]
    for n in active[1:]:
        most = jnp.maximum(most, n)
    lax.fori_loop(0, most, row, 0)
    size = trash // len(outs)
    copies = [
        pltpu.make_async_copy(obuf.at[pl.ds(i * size, size)], out, sems.at[i])
        for i, out in enumerate(outs)
    ]
    for copy in copies:
        copy.start()
    for copy in copies:
        copy.wait()


def add_kernel(nseg, nz, ny, nnz_a, offsets, meta, slots, here, *refs):
    chunks = len(offsets)
    got, out, bufs = refs[:chunks], refs[chunks], refs[chunks + 1 : 2 * chunks + 1]
    acc, stage, insems, sems = refs[2 * chunks + 1 :]
    cells = nz * ny
    for i in range(chunks):
        pltpu.make_async_copy(got[i], bufs[i], insems.at[i]).start()

    def clear(j, _):
        acc[pl.ds(j * 4, 4)] = jnp.zeros((4,) + acc.shape[1:], jnp.float32)
        return 0

    lax.fori_loop(0, acc.shape[0] // 4, clear, 0)
    low = lax.broadcasted_iota(jnp.int32, (BS, 2 * BS), 1) < BS
    z = here[0]
    for i in range(chunks):
        pltpu.make_async_copy(got[i], bufs[i], insems.at[i]).wait()
        for s, offset in enumerate(offsets[i]):
            zs = lax.rem(z + offset + nz, nz)

            def slot(j, _, i=i, s=s, zs=zs):
                y = j // 2
                c = zs * ny + y
                e = slots[2 * c + (j & 1)]

                @pl.when(e >= 0)
                def _():
                    base = cells * 128 + c * 128 + (e // 2) * 8
                    for k in range(nnz_a):
                        w = meta[base + k]
                        far = w & 63
                        seg = w >> 6
                        src = (far >> 4) * (cells * 128) + c * 128 + (far & 15) * 8 + 6
                        i0 = seg * cells + meta[src]
                        i1 = seg * cells + meta[src + 1]
                        x = bufs[i][y, 2 * s + (j & 1), :, 2 * BS * k : 2 * BS * (k + 1)]
                        x = x.astype(jnp.float32)
                        new0 = acc[i0] + jnp.where(low, x, 0.0)
                        new1 = acc[i1] + jnp.where(low, 0.0, x)
                        acc[i0] = new0
                        acc[i1] = new1

                return 0

            lax.fori_loop(0, 2 * ny, slot, 0)

    def put(seg, _):
        for h in range(cells // 2):
            a = acc[seg * cells + 2 * h]
            b = acc[seg * cells + 2 * h + 1]
            v = jnp.where(low, a, b) + pltpu.roll(jnp.where(low, b, a), BS, 1)
            stage[seg, :, 2 * BS * h : 2 * BS * (h + 1)] = v
        pltpu.make_async_copy(stage.at[seg], out.at[seg], sems.at[seg]).start()
        return 0

    lax.fori_loop(0, nseg, put, 0)

    def finish(seg, _):
        pltpu.make_async_copy(stage.at[seg], out.at[seg], sems.at[seg]).wait()
        return 0

    lax.fori_loop(0, nseg, finish, 0)


def last_kernel(nseg, nz, ny, nnz_a, offsets, offset, meta, slots, here, part, got, *refs):
    apart, out, acc, buf, late, stage, loadsems, sems = refs[:ny], *refs[ny:]
    cells = nz * ny
    loads = [pltpu.make_async_copy(part, acc, loadsems.at[0])]
    loads.append(pltpu.make_async_copy(got, buf, loadsems.at[1]))
    for i in range(ny):
        loads.append(pltpu.make_async_copy(apart[i], late.at[i], loadsems.at[2 + i]))
    for copy in loads:
        copy.start()
    for copy in loads:
        copy.wait()
    upper = lax.broadcasted_iota(jnp.int32, (BS, 2 * BS), 1) // BS
    z, y = here[0], here[1]

    def add(c, which, load):
        e = slots[2 * c + which]

        @pl.when(e >= 0)
        def _():
            base = cells * 128 + c * 128 + (e // 2) * 8
            for k in range(nnz_a):
                w = meta[base + k]
                far = w & 63
                seg = w >> 6
                src = (far >> 4) * (cells * 128) + c * 128 + (far & 15) * 8 + 6
                x = load(slice(2 * BS * k, 2 * BS * (k + 1))).astype(jnp.float32)
                turned_x = pltpu.roll(x, BS, 1)
                for q in range(2):
                    cell = meta[src + q]
                    side = cell & 1
                    lanes = pl.ds(pl.multiple_of((cell >> 1) * (2 * BS), 2 * BS), 2 * BS)
                    v = jnp.where(upper == side, jnp.where(side == q, x, turned_x), 0.0)
                    acc[seg, :, lanes] = acc[seg, :, lanes] + v

    for s, near in enumerate(offsets):
        zs = lax.rem(z + near + nz, nz)

        def slot(j, _, s=s, zs=zs):
            add(zs * ny + j // 2, j & 1, lambda cols: buf[j // 2, 2 * s + (j & 1), :, cols])
            return 0

        lax.fori_loop(0, 2 * ny, slot, 0)
    zs = lax.rem(z + offset + nz, nz)

    def slot(j, _):
        ys = lax.rem(y - j // 2 + ny, ny)
        add(zs * ny + ys, j & 1, lambda cols: late[j // 2, j & 1, :, cols])
        return 0

    lax.fori_loop(0, 2 * ny, slot, 0)

    def put(seg, _):
        stage[seg] = acc[seg].astype(jnp.bfloat16)
        pltpu.make_async_copy(stage.at[seg], out.at[seg], sems.at[seg]).start()
        return 0

    lax.fori_loop(0, nseg, put, 0)

    def finish(seg, _):
        pltpu.make_async_copy(stage.at[seg], out.at[seg], sems.at[seg]).wait()
        return 0

    lax.fori_loop(0, nseg, finish, 0)


def local(a_blocks, a_cols, p_blocks, p_cells):
    rows = a_blocks.shape[0]
    nnz_a = a_cols.shape[1]
    nz, ny = lax.axis_size("z"), lax.axis_size("y")
    cells = nz * ny
    frame, z, y = lax.axis_index("frame"), lax.axis_index("z"), lax.axis_index("y")
    coarse_here = rows // AGG
    nseg = coarse_here * 9
    half = nz // 2
    mid = rows // 2
    wide = 2 * nnz_a * BS

    p_ring, a_ring = [(p_blocks, p_blocks)], [(a_blocks, a_blocks)]
    for d in range(1, half + 1):
        up, down = p_ring[-1]
        p_ring.append(turned(up, None if d == half else down))
        up, down = a_ring[-1]
        if d == half:
            up, down = up[:mid], down[mid:]
        a_ring.append(turned(up, down))

    where_u = lax.div(a_cols, jnp.int32(rows * cells)) - frame + 1
    where_r = a_cols & (rows - 1)
    agg = jnp.arange(rows, dtype=jnp.int32)[:, None] // AGG
    seg = agg * 9 + where_u * 3 + where_r // AGG - agg + 1
    meta = jnp.concatenate([where_u * rows + where_r + 64 * seg, p_cells], axis=1).reshape(rows * 8)
    spread = jnp.broadcast_to(meta[None], (cells, rows * 8))
    spread, *beside = lax.optimization_barrier((spread, *p_ring[1]))
    everyone = lax.all_to_all(spread, ("z", "y"), 0, 0, tiled=True)
    mb, ma = shifted(everyone)
    three = jnp.stack([mb, everyone, ma]).reshape(-1)
    flat = everyone.reshape(-1)
    named = everyone.reshape(cells, rows, 8)[:, :, 6:].reshape(cells, 2 * rows)
    entry = jnp.arange(2 * rows, dtype=jnp.int32)[None]
    hit = named == z * ny + y
    first = jnp.min(jnp.where(hit, entry, 2 * rows), axis=1)
    last = jnp.max(jnp.where(hit, entry, -1), axis=1)
    slots = jnp.stack(
        [jnp.where(first < 2 * rows, first, -1), jnp.where(last > first, last, -1)], axis=1
    ).reshape(2 * cells)
    here = jnp.stack([z, y]).astype(jnp.int32)

    whole = (0, rows)
    whole = (0, rows)
    three_rings = zip((p_blocks,) + p_ring[1], (a_blocks,) + a_ring[1])
    p_list, a_list = zip(*three_rings)
    groups = [((0, -1, 1), tuple((i, *whole) for i in range(3)), a_list, p_list, 0, 0)]
    for d in range(2, half):
        groups.append(((-d, d), ((0, *whole), (1, *whole)), a_ring[d], p_ring[d], d - 1, 0))
    groups.append(((half,), ((0, 0, mid), (0, mid, mid)), a_ring[half], p_ring[half], 2, 2))
    batches = [
        (p_blocks, *beside),
        p_ring[2],
        p_ring[3] + p_ring[4],
    ]
    near = {}
    got = []
    for i, (offsets, pieces, a_list, p_list, batch, start) in enumerate(groups):
        if batch not in near:
            parts = batches[batch]
            if i == 2:
                *parts, sent = lax.optimization_barrier((*parts, sent))
            near[batch] = shifted(jnp.concatenate(parts, axis=0))
        if i > 0:
            if i > 1:
                sent, got[-1] = lax.optimization_barrier((sent, got[-1]))
            got.append(lax.all_to_all(sent, "y", 0, 0, tiled=True))
        pb, pa = near[batch]
        count = len(offsets)
        apart = i == len(groups) - 1
        parts_out = ny if apart else 1
        shape = (ny * 2 * count // parts_out, BS, wide)
        sent = pl.pallas_call(
            functools.partial(
                term_kernel, rows, nnz_a, nz, ny, offsets, pieces, start, apart
            ),
            out_shape=[jax.ShapeDtypeStruct(shape, jnp.bfloat16)] * parts_out,
            in_specs=[SMEM, SMEM] + [ANY] * (len(a_list) + len(p_list) + 2),
            out_specs=[ANY] * parts_out,
            scratch_shapes=[
                pltpu.VMEM((count, rows, BS, nnz_a * BS), jnp.bfloat16),
                pltpu.VMEM((count, 3 * rows, BS, 2 * BS), jnp.bfloat16),
                pltpu.VMEM((count, BS, wide), jnp.bfloat16),
                pltpu.VMEM((ny * 2 * count + 1, BS, wide), jnp.bfloat16),
                pltpu.SMEM((count * ny,), jnp.int32),
                pltpu.SMEM((count * (rows + 1),), jnp.int32),
                pltpu.SemaphoreType.DMA((len(pieces) + 3 * count + ny,)),
            ],
            compiler_params=pltpu.CompilerParams(vmem_limit_bytes=24 << 20),
            name="terms",
        )(flat, here, *a_list, *p_list, pb, pa)
        if apart:
            break
        sent = sent[0].reshape(ny, 2 * count, BS, wide)
    late = [sent[0]]
    for by in (1, 2, ny - 1):
        late.append(lax.ppermute(sent[by], "y", [(i, (i + by) % ny) for i in range(ny)]))
    offsets = [g[0] for g in groups]
    shape = (nseg, BS, cells * BS)
    early = got[:-1]
    part = pl.pallas_call(
        functools.partial(add_kernel, nseg, nz, ny, nnz_a, offsets[:-2]),
        out_shape=jax.ShapeDtypeStruct(shape, jnp.float32),
        in_specs=[SMEM, SMEM, SMEM] + [ANY] * len(early),
        out_specs=ANY,
        scratch_shapes=[pltpu.VMEM(g.shape, g.dtype) for g in early]
        + [
            pltpu.VMEM((nseg * cells, BS, 2 * BS), jnp.float32),
            pltpu.VMEM(shape, jnp.float32),
            pltpu.SemaphoreType.DMA((len(early),)),
            pltpu.SemaphoreType.DMA((nseg,)),
        ],
        compiler_params=pltpu.CompilerParams(vmem_limit_bytes=60 << 20),
        name="add",
    )(three, slots, here, *early)
    out = pl.pallas_call(
        functools.partial(last_kernel, nseg, nz, ny, nnz_a, offsets[-2], half),
        out_shape=jax.ShapeDtypeStruct(shape, jnp.bfloat16),
        in_specs=[SMEM, SMEM, SMEM] + [ANY] * (2 + ny),
        out_specs=ANY,
        scratch_shapes=[
            pltpu.VMEM(shape, jnp.float32),
            pltpu.VMEM(got[-1].shape, jnp.bfloat16),
            pltpu.VMEM((ny, 2, BS, wide), jnp.bfloat16),
            pltpu.VMEM(shape, jnp.bfloat16),
            pltpu.SemaphoreType.DMA((2 + ny,)),
            pltpu.SemaphoreType.DMA((nseg,)),
        ],
        compiler_params=pltpu.CompilerParams(vmem_limit_bytes=60 << 20),
        name="finish",
    )(three, slots, here, part, got[-1], *late)
    return out.reshape(coarse_here, 3, 3, BS, cells * BS)


def solution(mesh):
    frames = mesh.shape["frame"]
    grid = Mesh(mesh.devices.reshape(frames, 8, -1), ("frame", "z", "y"))
    dim = ("frame", "z", "y")

    return jax.shard_map(
        local,
        mesh=grid,
        in_specs=(P(dim, None, None), P(dim, None), P(dim, None, None), P(dim, None)),
        out_specs=P(dim, None, None, None, None),
        check_vma=False,
    )
```
